256 devices in a mesh: row: 16 (over y, x), col: 16 (over z, core).
Axes of the slice: x: 4, y: 4, z: 8, core: 2. Of those that a mesh axis runs over, the one named last changes fastest.
Arguments:
- amplitudes: float32 [128, 128, 6144], P('col', 'row'), may hold values from -6 to 6
- integrals: float32 [6144, 6144], P('col', 'row'), may hold values from -0.078125 to 0.078125
- amp_pattern: int32 [128, 48], P('col'), may hold values 0 or 1
- int_pattern: int32 [48, 48], P(None, 'row'), may hold values from 0 to 1
Outputs:
- ladder: float32 [128, 128, 6144], P('col', 'row')
The draws below stay inside these ranges and needn't reach their ends.
All inputs are finite; a program needn't handle non-finite values. No bound on the sum of `amp_pattern` on one device may be relied on, other than what follows from the above.
Results may differ from the reference program's by a relative error of at most 0.00007.
Values sent between devices are 32-bit elements; how exact they have to be, the bound alone decides.
A program may use at most 128 MiB of HBM per device.

```python
import jax
import jax.numpy as jnp
from jax import lax

OCC = 128
TILE = 128
KTILES = 48
NTILES = 48
KDIM = 6144
NDIM = 6144


def draw_int_pattern(key, part):
    tile_index = lax.broadcasted_iota(jnp.int32, (KTILES, NTILES), 1)
    drawn = jax.random.randint(key, (KTILES, NTILES), 0, NTILES)
    return (drawn <= tile_index).astype(jnp.int32)


def set_ends(values, key, least, largest):
    longest = values.shape.index(max(values.shape))
    spots = []
    for shift in (0, 1):
        where = [jax.random.randint(jax.random.fold_in(key, axis), (), 0, length) for axis, length in enumerate(values.shape)]
        where[longest] = (where[longest] + shift) % values.shape[longest]
        spots.append(tuple(where))
    return values.at[spots[0]].set(least).at[spots[1]].set(largest)


def levels(stream_key, extent, split, smallest, top_value):
    factor_of = 1.0
    for position, shards_of in split:
        draws = jax.random.uniform(jax.random.fold_in(jax.random.fold_in(stream_key, 6), position), (shards_of,), jnp.float32, smallest / len(split), top_value / len(split))
        factor_of = factor_of * jnp.repeat(jnp.exp(draws), extent[position] // shards_of).reshape((-1,) + (1,) * (len(extent) - 1 - position))
    return factor_of


def normal_values(key, shape, scale, limit, shards=(), dtype=jnp.bfloat16):
    gain = levels(key, shape, shards, -0.22, 0.18) if shards else 1.0
    values = jax.random.normal(key, shape, jnp.float32) * scale * gain
    return jnp.minimum(jnp.maximum(values, -limit), limit).astype(dtype)


def setup_inputs(seed: int = 0) -> dict:
    seeds = jax.random.split(jax.random.key(seed), 5)
    amplitudes = normal_values(seeds[0], (OCC, OCC, KDIM), 1.0, 6.0, ((0, 16), (1, 16)), jnp.float32)
    integrals = normal_values(seeds[1], (KDIM, NDIM), KDIM ** -0.5, 0.078125, ((0, 16), (1, 16)), jnp.float32)
    amp_pattern = set_ends((jax.random.randint(seeds[2], (OCC, KTILES), 0, 2) < 1).astype(jnp.int32), jax.random.fold_in(seeds[2], 1), 0, 1)
    int_pattern = draw_int_pattern(jax.random.fold_in(seeds[4], 71), 0)
    return {"amplitudes": amplitudes, "integrals": integrals, "amp_pattern": amp_pattern, "int_pattern": int_pattern}


def reference(amplitudes, integrals, amp_pattern, int_pattern):
    amp_mask = amp_pattern.astype(jnp.float32)
    int_mask = int_pattern.astype(jnp.float32)
    sparse_amp = (amplitudes.reshape(OCC, OCC, KTILES, TILE) * amp_mask[:, None, :, None]).reshape(OCC, OCC, KDIM)
    sparse_int = (integrals.reshape(KTILES, TILE, NTILES, TILE) * int_mask[:, None, :, None]).reshape(KDIM, NDIM)

    def one_index(block):
        return jnp.dot(block, sparse_int, precision=lax.Precision.HIGHEST, preferred_element_type=jnp.float32)

    return lax.map(one_index, sparse_amp)
```

```python
import jax
import jax.numpy as jnp
from jax import lax
from jax.experimental import pallas as pl
from jax.experimental.pallas import tpu as pltpu
from jax.sharding import PartitionSpec as P

TILE = 128
MESH = pl.DeviceIdType.MESH
SX, SY, SZ = 4, 4, 8
CUT = 152
A1, B1, A2, B2, XA, LA = range(6)

PROGRAM = (
        (769, 1153, 777, 1161, 897, 1025, 905, 1033, 641, 1281, 1289, 657, 1297, 1305, 673, 1313, 1321, 1, 770, 1041,
     1049, 129, 1177, 513, 1282, 689, 1337, 1169, 137, 1273, 898, 906, 529, 1298, 705, 1353, 1265, 257, 1026, 265,
     1034, 1329, 721, 1369, 514, 521,),
        (545, 1314, 737, 1385, 530, 537,),
        (385, 1154, 9, 1073, 1081, 130, 1193, 1345, 753, 1401, 138, 1257, 899, 907, 561, 1330, 546, 553,),
        (1185, 258, 1027, 266, 1035, 1361, 577, 1346, 562, 569,),
        (1377, 1249, 593, 1362, 273, 1042, 281, 1050, 578, 585,),
        (1393, 131, 1209, 139, 1241, 609, 1378, 1201, 900, 313, 1082, 259, 594, 601,),
        (625, 1394, 267, 610, 617,),
        (1028, 2, 1065, 1233, 282, 1051, 305, 1074, 401, 1170, 132, 1225, 314, 1083, 274, 1043, 260, 626, 633,),
        (1217, 297, 1066,),
        (393,),
        (),
        (1057, 409,),
        (497,),
        (1266, 505,),
        (417,),
        (306, 425,),
        (1186, 1075, 481,),
        (489,),
        (275, 433,),
        (1044, 298, 1067, 1250, 1202, 289, 1058, 307, 441,),
        (283, 465,),
        (1076, 315, 473,),
        (1234, 276, 449,),
        (290, 1059, 1218, 308, 457,),
        (386,),
        (402,),
        (291, 1060, 498,),
        (418,),
        (482,),
        (434,),
        (299, 466,),
        (292, 450,),
)


def decode(code):
    code, hop = divmod(code, 8)
    code, direction = divmod(code, 2)
    code, index = divmod(code, 8)
    op, kind = divmod(code, 6)
    return op, (kind, index, direction, hop)


STEPS = tuple(tuple(decode(code) for code in group) for group in PROGRAM)
MESSAGES = tuple(sorted({m for group in STEPS for op, m in group if op == 1}))
IDS = {m: n for n, m in enumerate(MESSAGES)}


def place(direction, hop, size):
    return hop if direction == 0 else (size - hop) % size


def kernel(a_ref, v_ref, out_ref, vg, ag, ah, al, acc, rb, fin, send, recv, lsem, ssend, srecv, r1s, r1r, r2s, r2r, vsem):
    row, col = lax.axis_index("row"), lax.axis_index("col")
    y, x = row // SX, row % SX
    z, k = col // 2, col % 2
    s = 1 - 2 * k
    rows, width = v_ref.shape

    def device(dx=0, dy=0, dz=0):
        return (((y - s * dy + SY) % SY) * SX + (x - s * dx + SX) % SX, ((z - s * dz + SZ) % SZ) * 2 + k)

    sibling = (row, z * 2 + 1 - k)

    barrier = pltpu.get_barrier_semaphore()
    partners = [sibling] + [device(dx=d) for d in (1, 2, 3)] + [device(dy=d) for d in (1, 3)] + [device(dz=d) for d in (1, 7)]
    for partner in partners:
        pl.semaphore_signal(barrier, inc=1, device_id=partner, device_id_type=MESH)
    pl.semaphore_wait(barrier, len(partners))

    first, last = pl.ds(0, CUT), pl.ds(CUT, rows - CUT)

    def message(m):
        kind, index, direction, hop = m
        step = 1 if direction == 0 else -1
        if kind == XA:
            source, target = ag.at[index, place(direction, hop - 1, SX)], ag.at[index, place(direction, hop, SX)]
            to = device(dx=-step)
        elif kind == A1:
            source, target = vg.at[place(direction, hop - 1, SY), 0, first], vg.at[place(direction, hop, SY), 0, first]
            to = device(dy=-step)
        elif kind == B2:
            source = vg.at[place(direction, hop - 1, SY), index, last]
            target = vg.at[place(direction, hop, SY), index, last]
            to = device(dy=-step)
        else:
            part = last if kind == B1 else first
            source, target = vg.at[index, place(direction, hop - 1, SZ), part], vg.at[index, place(direction, hop, SZ), part]
            to = device(dz=-step)
        if hop == 1 and kind in (A1, B1, A2, B2) and index == 0:
            source = v_ref.at[first if kind in (A1, A2) else last]
        number = IDS[m]
        return pltpu.make_async_remote_copy(
            src_ref=source, dst_ref=target, send_sem=send.at[number], recv_sem=recv.at[number], device_id=to, device_id_type=MESH
        )

    def block(j, sense):
        sign = 1 - 2 * (j % 2)
        return (z + sense * sign * ((j + 1) // 2) + SZ) % SZ

    def columns(start):
        return pl.ds(pl.multiple_of(start * width, width), width)

    def own(j):
        return pltpu.make_async_copy(a_ref.at[:, columns(2 * block(j, s) + k)], ag.at[j, 0, 0], lsem.at[j])

    def other(j):
        return pltpu.make_async_remote_copy(
            src_ref=a_ref.at[:, columns(2 * block(j, -s) + 1 - k)],
            dst_ref=ag.at[j, 0, 1],
            send_sem=ssend.at[j],
            recv_sem=srecv.at[j],
            device_id=sibling,
            device_id_type=MESH,
        )

    def run(entry):
        op, m = entry
        if op == 1:
            message(m).start()
        elif m[0] == LA:
            own(m[1]).wait()
            other(m[1]).wait_recv()
        else:
            message(m).wait_recv()

    def half(d):
        return pltpu.make_async_remote_copy(
            src_ref=acc.at[d, :, 1],
            dst_ref=rb.at[(SY - d) % SY],
            send_sem=r1s.at[d],
            recv_sem=r1r.at[(SY - d) % SY],
            device_id=sibling,
            device_id_type=MESH,
        )

    def half_in(d):
        return pltpu.make_async_remote_copy(
            src_ref=acc.at[d, :, 1], dst_ref=rb.at[d], send_sem=r1s.at[d], recv_sem=r1r.at[d], device_id=sibling, device_id_type=MESH
        )

    def result(d, dx):
        return pltpu.make_async_remote_copy(
            src_ref=fin.at[d, dx],
            dst_ref=out_ref.at[:, columns((y - s * d + SY) % SY * SX + x)],
            send_sem=r2s.at[d, dx],
            recv_sem=r2r.at[d, dx],
            device_id=device(dx=dx),
            device_id_type=MESH,
        )

    def finish(d):
        half_in(d).wait_recv()
        for dx in (2, 1, 3, 0):
            total = acc[d, dx, 0] + rb[d, (SX - dx) % SX]
            if dx == 0:
                out_ref[:, columns((y - s * d + SY) % SY * SX + x)] = total
            else:
                fin[d, dx] = total
        for dx in (2, 1, 3):
            result(d, dx).start()

    mine = pltpu.make_async_copy(v_ref, vg.at[0, 0], vsem)
    for j in range(SZ):
        own(j).start()
        other(j).start()
    early = [entry for entry in STEPS[0] if entry[0] == 1 and entry[1][3] == 1 and (entry[1][0] in (A1, B1) or entry[1][1] == 0)]
    early = [entry for entry in early if entry[1][0] != XA]
    for entry in early:
        run(entry)
    mine.start()
    acc[...] = jnp.zeros_like(acc)
    mine.wait()

    @pl.loop(0, 4 * SZ)
    def _(t):
        for number, group in enumerate(STEPS):
            todo = [entry for entry in group if number > 0 or entry not in early]
            if todo:

                @pl.when(t == number)
                def _():
                    for entry in todo:
                        run(entry)

        middle = t - SZ
        inner = jnp.logical_and(t >= SZ, t < 3 * SZ)
        j = jnp.where(inner, middle // 2, t % SZ)
        dy = jnp.where(inner, 1 + 2 * (middle % 2), jnp.where(t < SZ, 0, 2))
        dz = ((j % 2) * ((j + 1) // 2) + (1 - j % 2) * (SZ - (j + 1) // 2)) % SZ

        @pl.when(t < SZ)
        def _():
            value = ag[j].reshape(SX * 2 * a_ref.shape[0], width)
            high = value.astype(jnp.bfloat16)
            ah[j] = high
            al[j] = (value - high.astype(jnp.float32)).astype(jnp.bfloat16)

        value = vg[dy, dz]
        high = value.astype(jnp.bfloat16)
        low = (value - high.astype(jnp.float32)).astype(jnp.bfloat16)
        a_high, a_low = ah[j], al[j]
        product = jnp.dot(a_high, high, preferred_element_type=jnp.float32)
        product += jnp.dot(a_high, low, preferred_element_type=jnp.float32)
        product += jnp.dot(a_low, high, preferred_element_type=jnp.float32)
        acc[dy] += product.reshape(acc.shape[1:])

        for number, todo in ((7, ((half, 0),)), (9, ((finish, 0),)), (23, ((half, 1), (half, 3))), (25, ((finish, 1), (finish, 3)))):

            @pl.when(t == number)
            def _():
                for what, d in todo:
                    what(d).start() if what is half else what(d)

    half(2).start()
    finish(2)

    for d in range(SY):
        half(d).wait_send()
        for dx in (1, 2, 3):
            result(d, dx).wait()
    for j in range(SZ):
        other(j).wait_send()
    for m in MESSAGES:
        message(m).wait_send()


def body(amplitudes, integrals, amp_pattern, int_pattern):
    first, second, depth = amplitudes.shape
    rows, width = integrals.shape
    ktiles = amp_pattern.shape[1]
    masked = amplitudes.reshape(first, second, ktiles, TILE) * amp_pattern.astype(jnp.float32)[:, None, :, None]
    masked = masked.reshape(first * second, depth)
    tiles = rows // TILE
    here = lax.dynamic_slice_in_dim(int_pattern, lax.axis_index("col") * tiles, tiles, 0).astype(jnp.float32)
    shaped = integrals.reshape(tiles, TILE, width // TILE, TILE) * here[:, None, :, None]
    shaped = shaped.reshape(rows, width)
    pairs = first * second
    f32, bf16 = jnp.float32, jnp.bfloat16
    dma = pltpu.SemaphoreType.DMA
    out = pl.pallas_call(
        kernel,
        out_shape=jax.ShapeDtypeStruct((pairs, depth), f32),
        in_specs=[pl.BlockSpec(memory_space=pltpu.VMEM)] * 2,
        out_specs=pl.BlockSpec(memory_space=pltpu.VMEM),
        scratch_shapes=[
            pltpu.VMEM((SY, SZ, rows, width), f32),
            pltpu.VMEM((SZ, SX, 2, pairs, width), f32),
            pltpu.VMEM((SZ, SX * 2 * pairs, width), bf16),
            pltpu.VMEM((SZ, SX * 2 * pairs, width), bf16),
            pltpu.VMEM((SY, SX, 2, pairs, width), f32),
            pltpu.VMEM((SY, SX, pairs, width), f32),
            pltpu.VMEM((SY, SX, pairs, width), f32),
            dma((len(MESSAGES),)),
            dma((len(MESSAGES),)),
            dma((SZ,)),
            dma((SZ,)),
            dma((SZ,)),
            dma((SY,)),
            dma((SY,)),
            dma((SY, SX)),
            dma((SY, SX)),
            dma,
        ],
        compiler_params=pltpu.CompilerParams(collective_id=0, has_side_effects=True, vmem_limit_bytes=60000 * 1024),
    )(masked, shaped)
    return out.reshape(first, second, depth)


def solution(mesh):
    placed = (P("col", "row", None), P("col", "row"), P("col", None), P(None, "row"))
    return jax.shard_map(
        body, mesh=mesh, in_specs=placed, out_specs=P("col", "row", None), check_vma=False
    )
```

```python
import jax
import jax.numpy as jnp
from jax import lax
from jax.experimental import pallas as pl
from jax.experimental.pallas import tpu as pltpu
from jax.sharding import PartitionSpec as P

TILE = 128
MESH = pl.DeviceIdType.MESH
RING, SZ, SETS, HELD = 4, 8, 4, 2
PARTS = 2
B1, B2, XA, LA, XE = range(5)

PROGRAM = (
    (769, 777, 773, 781, 1152, 1153, 645, 653, 641, 1160, 385, 897, 901, 129, 770, 5, 817, 821, 257, 898, 1161, 137,
     778, 1, 789, 649, 1176, 258, 261,),
    (393, 905, 909,),
    (785, 133, 141,),
    (13, 829, 1177, 825, 642, 9, 797, 130, 138,),
    (265, 906, 409, 921, 925, 1168, 793, 1169, 650, 2, 805, 401, 917, 913, 801, 266, 269,),
    (149, 157,),
    (145, 786, 10, 813, 153,),
    (281, 922, 809, 273, 914, 794, 282, 285,),
    (177, 818, 185,),
    (826, 181, 189,),
    (274, 277,),
    (161, 802, 169,),
    (165, 173,),
    (810, 146, 154,),
    (178, 186,),
    (162, 170,),
)
ORDER = ((0, 0), (1, 0), (3, 0), (2, 0), (0, 1), (3, 1), (1, 1), (0, 3), (1, 3), (3, 3), (0, 2), (1, 2), (3, 2), (2, 1), (2, 3), (2, 2))
AFTER = (
    (),
    (),
    (),
    (),
    (),
    (),
    (),
    (),
    (),
    (),
    ((0, 0),),
    ((1, 0),),
    ((0, 1), (0, 3), (2, 0)),
    ((1, 1), (1, 3)),
    ((2, 1), (2, 3)),
    ((0, 2), (1, 2), (2, 2)),
)


def decode(code):
    code, hop = divmod(code, 4)
    code, direction = divmod(code, 2)
    code, index = divmod(code, 16)
    op, kind = divmod(code, 5)
    return op, (kind, index, direction, hop)


STEPS = tuple(tuple(decode(code) for code in group) for group in PROGRAM)
MESSAGES = tuple(sorted({m for group in STEPS for op, m in group if op == 1 and m[0] != XE}))
IDS = {m: n for n, m in enumerate(MESSAGES)}
FIRST = {}
for step, (_, block) in enumerate(ORDER):
    FIRST.setdefault(block, step)


def place(direction, hop):
    return hop if direction == 0 else (RING - hop) % RING


def split(value):
    high = value.astype(jnp.bfloat16)
    return high, (value - high.astype(jnp.float32)).astype(jnp.bfloat16)


def choose(t, values):
    chosen = jnp.int32(values[0])
    for number, value in enumerate(values[1:], 1):
        chosen = jnp.where(t == number, value, chosen)
    return chosen


def kernel(a_ref, v_ref, out_ref, vg, ag, ah, al, acc, rb, zs, zr, fin, send, recv, lsem, xes, xer, r1s, r1r, r2s, r2r, r3s, r3r, vsem):
    row, col = lax.axis_index("row"), lax.axis_index("col")
    y, x = row // RING, row % RING
    z, k = col // 2, col % 2
    s = 1 - 2 * k
    rows, width = v_ref.shape
    piece = rows // PARTS

    def device(dx=0, dy=0, dz=0, core=k):
        return (((y - s * dy + RING) % RING) * RING + (x - s * dx + RING) % RING, ((z - s * dz + SZ) % SZ) * 2 + core)

    sibling = device(core=1 - k)
    ahead, behind, across = device(dz=-1), device(dz=1), device(dz=-1, core=1 - k)

    barrier = pltpu.get_barrier_semaphore()
    partners = [sibling, ahead, behind, across, device(dz=2), device(dz=-2)]
    partners += [device(dx=d) for d in (1, 2, 3)] + [device(dy=d) for d in (1, 3)]
    for partner in partners:
        pl.semaphore_signal(barrier, inc=1, device_id=partner, device_id_type=MESH)
    pl.semaphore_wait(barrier, len(partners))

    def remote(source, target, send_sem, recv_sem, to):
        return pltpu.make_async_remote_copy(
            src_ref=source, dst_ref=target, send_sem=send_sem, recv_sem=recv_sem, device_id=to, device_id_type=MESH
        )

    def message(m):
        kind, index, direction, hop = m
        step = 1 if direction == 0 else -1
        here, there = place(direction, hop - 1), place(direction, hop)
        if kind == XA:
            source, target, to = ag.at[index, here], ag.at[index, there], device(dx=-step)
        elif kind == B2:
            block, part = index // PARTS, pl.ds(index % PARTS * piece, piece)
            source, target, to = vg.at[here, block, part], vg.at[there, block, part], device(dy=-step)
            if hop == 1 and block == 0:
                source = v_ref.at[part]
        else:
            part = pl.ds(index * piece, piece)
            source, target, to = vg.at[0, here, part], vg.at[0, there, part], device(dz=-2 * step)
            if hop == 1:
                source = v_ref.at[part]
        return remote(source, target, send.at[IDS[m]], recv.at[IDS[m]], to)

    def columns(start):
        return pl.ds(pl.multiple_of(start * width, width), width)

    def block_of(owner, sense, core, j):
        return a_ref.at[:, columns(2 * ((owner - sense * 2 * j + 2 * SZ) % SZ) + core)]

    def own(j):
        return pltpu.make_async_copy(block_of(z, s, k, j), ag.at[j, 0, 0], lsem.at[j])

    def give(j, way):
        owner = z + s if way < 2 else z
        slot = (1, 3, 2)[way]
        sense, core = (s, k) if way == 0 else (-s, 1 - k)
        to = (ahead, across, sibling)[way]
        return remote(block_of(owner, sense, core, j), ag.at[j, 0, slot], xes.at[j, way], xer.at[j, way], to)

    def run(entry):
        op, m = entry
        if m[0] == XE:
            give(m[1], m[3]).start()
        elif op == 1:
            message(m).start()
        elif m[0] == LA:
            own(m[1]).wait()
            for way in (0, 1, 2):
                give(m[1], way).wait_recv()
        else:
            message(m).wait_recv()

    def core_half(d, there):
        return remote(acc.at[d, :, HELD:SETS], rb.at[there], r1s.at[d], r1r.at[there], sibling)

    def z_half(d):
        return remote(zs.at[d], zr.at[d], r2s.at[d], r2r.at[d], behind)

    def here(d):
        return columns((y - s * d + RING) % RING * RING + x)

    def result(d, dx):
        return remote(fin.at[d, dx], out_ref.at[:, here(d)], r3s.at[d, dx], r3r.at[d, dx], device(dx=dx))

    def stage(number, d):
        if number == 0:
            core_half(d, (RING - d) % RING).start()
        elif number == 1:
            core_half(d, d).wait_recv()
            for dx in range(RING):
                zs[d, dx] = acc[d, dx, 1] + rb[d, (RING - dx) % RING, 1]
            for dx in range(RING):
                fin[d, dx] = acc[d, dx, 0] + rb[d, (RING - dx) % RING, 0]
            z_half(d).start()
        else:
            z_half(d).wait_recv()
            for dx in (2, 1, 3, 0):
                total = fin[d, dx] + zr[d, dx]
                if dx == 0:
                    out_ref[:, here(d)] = total
                else:
                    fin[d, dx] = total
            for dx in (2, 1, 3):
                result(d, dx).start()

    mine = pltpu.make_async_copy(v_ref, vg.at[0, 0], vsem)
    early = [entry for entry in STEPS[0] if entry[0] == 1 and (entry[1][0] == XE or (entry[1][0] == B1 and entry[1][3] == 1))]
    early += [entry for entry in STEPS[0] if entry[0] == 1 and entry[1][0] == B2 and entry[1][3] == 1 and entry[1][1] < PARTS]
    for entry in early:
        run(entry)
    for j in range(RING):
        own(j).start()
        give(j, 2).start()
    mine.start()
    acc[...] = jnp.zeros_like(acc)
    mine.wait()

    @pl.loop(0, len(ORDER))
    def _(t):
        for number, group in enumerate(STEPS):
            todo = [entry for entry in group if number > 0 or entry not in early]
            if todo:

                @pl.when(t == number)
                def _():
                    for entry in todo:
                        run(entry)

        dy, j = choose(t, [d for d, _ in ORDER]), choose(t, [b for _, b in ORDER])
        fresh = t == FIRST[0]
        for b in range(1, RING):
            fresh = jnp.logical_or(fresh, t == FIRST[b])

        @pl.when(fresh)
        def _():
            ah[j], al[j] = split(ag[j].reshape(ah.shape[1:]))

        high, low = split(vg[dy, j])
        product = jnp.dot(ah[j], high, preferred_element_type=jnp.float32)
        product += jnp.dot(ah[j], low, preferred_element_type=jnp.float32)
        product += jnp.dot(al[j], high, preferred_element_type=jnp.float32)
        acc[dy] += product.reshape(acc.shape[1:])

        for number, group in enumerate(AFTER[:-1]):
            if group:

                @pl.when(t == number)
                def _():
                    for what in group:
                        stage(*what)

    for what in AFTER[-1]:
        stage(*what)

    for d in range(RING):
        core_half(d, d).wait_send()
        z_half(d).wait_send()
        for dx in (1, 2, 3):
            result(d, dx).wait()
    for j in range(RING):
        for way in (0, 1, 2):
            give(j, way).wait_send()
    for m in MESSAGES:
        message(m).wait_send()


def body(amplitudes, integrals, amp_pattern, int_pattern):
    first, second, depth = amplitudes.shape
    rows, width = integrals.shape
    ktiles = amp_pattern.shape[1]
    masked = amplitudes.reshape(first, second, ktiles, TILE) * amp_pattern.astype(jnp.float32)[:, None, :, None]
    masked = masked.reshape(first * second, depth)
    tiles = rows // TILE
    here = lax.dynamic_slice_in_dim(int_pattern, lax.axis_index("col") * tiles, tiles, 0).astype(jnp.float32)
    shaped = integrals.reshape(tiles, TILE, width // TILE, TILE) * here[:, None, :, None]
    shaped = shaped.reshape(rows, width)
    pairs = first * second
    f32, bf16 = jnp.float32, jnp.bfloat16
    dma = pltpu.SemaphoreType.DMA
    out = pl.pallas_call(
        kernel,
        out_shape=jax.ShapeDtypeStruct((pairs, depth), f32),
        in_specs=[pl.BlockSpec(memory_space=pltpu.VMEM)] * 2,
        out_specs=pl.BlockSpec(memory_space=pltpu.VMEM),
        scratch_shapes=[
            pltpu.VMEM((RING, RING, rows, width), f32),
            pltpu.VMEM((RING, RING, SETS, pairs, width), f32),
            pltpu.VMEM((RING, RING * SETS * pairs, width), bf16),
            pltpu.VMEM((RING, RING * SETS * pairs, width), bf16),
            pltpu.VMEM((RING, RING, SETS, pairs, width), f32),
            pltpu.VMEM((RING, RING, HELD, pairs, width), f32),
            pltpu.VMEM((RING, RING, pairs, width), f32),
            pltpu.VMEM((RING, RING, pairs, width), f32),
            pltpu.VMEM((RING, RING, pairs, width), f32),
            dma((len(MESSAGES),)),
            dma((len(MESSAGES),)),
            dma((RING,)),
            dma((RING, 3)),
            dma((RING, 3)),
            dma((RING,)),
            dma((RING,)),
            dma((RING,)),
            dma((RING,)),
            dma((RING, RING)),
            dma((RING, RING)),
            dma,
        ],
        compiler_params=pltpu.CompilerParams(collective_id=0, has_side_effects=True, vmem_limit_bytes=60000 * 1024),
    )(masked, shaped)
    return out.reshape(first, second, depth)


def solution(mesh):
    placed = (P("col", "row", None), P("col", "row"), P("col", None), P(None, "row"))
    return jax.shard_map(
        body, mesh=mesh, in_specs=placed, out_specs=P("col", "row", None), check_vma=False
    )
```

```python
import jax
import jax.numpy as jnp
from jax import lax
from jax.experimental import pallas as pl
from jax.experimental.pallas import tpu as pltpu
from jax.sharding import PartitionSpec as P

TILE = 128
MESH = pl.DeviceIdType.MESH
RING, SZ = 4, 8
PARTS = 2
B1, B2, B3, XA, LA, XE = range(6)
FULL, WIDE, NARROW = (0, 384), (0, 256), (256, 128)
SPANS = (FULL, WIDE, NARROW)
UNITS = ((0, FULL), (1, FULL), (3, FULL), (2, WIDE), (2, NARROW))

PROGRAM = (
    (1153, 1161, 1157, 1165, 1025, 1664, 1668, 1029, 1037, 512, 1409, 1413, 528, 1425, 1429, 560, 1457, 1461, 544,
     1441, 1445, 385, 1410, 1672, 401, 1426, 1, 1169, 5, 1201, 129, 137, 1282, 1173, 1205, 1676, 1688, 433, 1458,
     520, 1421, 1692, 1290, 1680, 1417, 536, 1437, 1684, 1033, 1026, 1433, 13, 1209, 1213, 568, 1469, 552, 1453,
     1465, 417, 1442, 9, 1177, 1181, 1034, 393, 1418, 409, 1434, 441, 1466, 2, 1185, 1189, 1449, 386, 389, 394,
     397,),
    (177, 185, 1330,),
    (10, 1197, 402, 405, 410, 413,),
    (1193, 434, 437, 442, 445,),
    (425, 1450, 133, 141,),
    (145, 153,),
    (149, 157,),
    (1298, 418, 421, 426, 429,),
    (2048,),
    (1306, 181, 189,),
    (2176, 165, 173,),
    (2064, 1338, 258,),
    (161, 169,),
    (2056, 306,),
    (2304, 2184, 1314, 1322, 274,),
    (2192, 266,),
    (282,),
    (314,),
    (2312, 290,),
    (2072, 2320, 298,),
    (2080, 2200, 2208, 2328, 2336,),
)
ORDER = ((0, 0, 0), (0, 1, 0), (0, 0, 1), (0, 0, 3), (0, 3, 0), (0, 1, 1), (0, 3, 1), (0, 0, 2), (0, 1, 3), (0, 3,
    3), (0, 3, 2), (1, 2, 0), (0, 1, 2), (1, 2, 3), (1, 2, 1), (2, 2, 0), (2, 2, 1), (2, 2, 3), (1, 2, 2), (2, 2,
    2))


def decode(code):
    code, hop = divmod(code, 4)
    code, direction = divmod(code, 2)
    code, index = divmod(code, 16)
    op, kind = divmod(code, 8)
    return op, (kind, index, direction, hop)


STEPS = tuple(tuple(decode(code) for code in group) for group in PROGRAM)
MESSAGES = tuple(sorted({m for group in STEPS for op, m in group if op == 1 and m[0] != XE}))
IDS = {m: n for n, m in enumerate(MESSAGES)}


def firsts(values):
    return tuple(min(n for n, v in enumerate(values) if v == value) for value in sorted(set(values)))


FRESH = firsts([b for _, _, b in ORDER])


def place(direction, hop):
    return hop if direction == 0 else (RING - hop) % RING


def split(value):
    high = value.astype(jnp.bfloat16)
    return high, (value - high.astype(jnp.float32)).astype(jnp.bfloat16)


def choose(t, values):
    chosen = jnp.int32(values[0])
    for number, value in enumerate(values[1:], 1):
        if value != values[number - 1]:
            chosen = jnp.where(t >= number, value, chosen)
    return chosen


def among(t, numbers):
    found = t == numbers[0]
    for number in numbers[1:]:
        found = jnp.logical_or(found, t == number)
    return found


def kernel(
    amp_ref, int_ref, a_ref, v_ref, out_ref, am, vg, ag, ah, al, acc, rb, zs, zr, fin,
    send, recv, lsem, xes, xer, r1s, r1r, r2s, r2r, r3s, r3r,
):
    row, col = lax.axis_index("row"), lax.axis_index("col")
    y, x = row // RING, row % RING
    z, k = col // 2, col % 2
    s = 1 - 2 * k
    first, second, depth = a_ref.shape
    rows, width = v_ref.shape
    pairs = first * second
    tiles = rows // TILE
    piece = rows // PARTS

    def device(dx=0, dy=0, dz=0, core=k):
        return (((y - s * dy + RING) % RING) * RING + (x - s * dx + RING) % RING, ((z - s * dz + SZ) % SZ) * 2 + core)

    sibling = device(core=1 - k)
    ahead, behind, across = device(dz=-1), device(dz=1), device(dz=-1, core=1 - k)

    barrier = pltpu.get_barrier_semaphore()
    partners = [sibling, ahead, behind, across, device(dz=2), device(dz=-2)]
    partners += [device(dx=d) for d in (1, 2, 3)] + [device(dy=d) for d in (1, 3)]
    for partner in partners:
        pl.semaphore_signal(barrier, inc=1, device_id=partner, device_id_type=MESH)

    for r in range(tiles):
        for c in range(width // TILE):
            part = (pl.ds(r * TILE, TILE), pl.ds(c * TILE, TILE))
            vg[0, 0, part[0], part[1]] = v_ref[part] * int_ref[col * tiles + r, c].astype(jnp.float32)

    @pl.loop(0, depth // TILE)
    def _(tile):
        part = pl.ds(pl.multiple_of(tile * TILE, TILE), TILE)
        for i in range(first):
            am[i, :, part] = a_ref[i, :, part] * amp_ref[i, tile].astype(jnp.float32)

    pl.semaphore_wait(barrier, len(partners))

    def remote(source, target, send_sem, recv_sem, to):
        return pltpu.make_async_remote_copy(
            src_ref=source, dst_ref=target, send_sem=send_sem, recv_sem=recv_sem, device_id=to, device_id_type=MESH
        )

    def message(m):
        kind, index, direction, hop = m
        step = 1 if direction == 0 else -1
        here, there = place(direction, hop - 1), place(direction, hop)
        if kind == XA:
            block, foreign = index // 2, index % 2
            source, target, to = ag.at[block, here, foreign], ag.at[block, there, foreign], device(dx=-step)
        elif kind == B1:
            part = pl.ds(index * piece, piece)
            source, target, to = vg.at[0, here, part], vg.at[0, there, part], device(dz=-2 * step)
        elif kind == B2:
            block, part = index // PARTS, pl.ds(index % PARTS * piece, piece)
            source, target, to = vg.at[here, block, part], vg.at[there, block, part], device(dy=-step)
        else:
            block, span = index // 2, pl.ds(*SPANS[1 + index % 2])
            source, target, to = vg.at[here, block, :, span], vg.at[there, block, :, span], device(dy=-step)
        return remote(source, target, send.at[IDS[m]], recv.at[IDS[m]], to)

    def columns(start, offset=0, size=None):
        return pl.ds(pl.multiple_of(start * width + offset, TILE), size or width)

    def block_of(owner, sense, core, j):
        return am.at[:, :, columns(2 * ((owner - sense * 2 * j + 2 * SZ) % SZ) + core)]

    def own(j):
        return pltpu.make_async_copy(block_of(z, s, k, j), ag.at[j, 0, 0, 0], lsem.at[j])

    def give(j, way):
        owner = z + s if way < 2 else z
        slot = ((1, 0), (1, 1), (0, 1))[way]
        sense, core = (s, k) if way == 0 else (-s, 1 - k)
        to = (ahead, across, sibling)[way]
        return remote(block_of(owner, sense, core, j), ag.at[(j, 0) + slot], xes.at[j, way], xer.at[j, way], to)

    def core_half(u, there):
        d, span = UNITS[u]
        span = pl.ds(*span)
        return remote(acc.at[d, :, :, 1, :, span], rb.at[UNITS[there][0], :, :, :, span], r1s.at[u], r1r.at[there], sibling)

    def z_half(u):
        d, span = UNITS[u]
        span = pl.ds(*span)
        return remote(zs.at[d, :, :, span], zr.at[d, :, :, span], r2s.at[u], r2r.at[u], behind)

    def home(u):
        d, span = UNITS[u]
        return columns((y - s * d + RING) % RING * RING + x, *span)

    def result(u, dx):
        d, span = UNITS[u]
        return remote(fin.at[d, dx, :, :, pl.ds(*span)], out_ref.at[:, :, home(u)], r3s.at[u, dx], r3r.at[u, dx], device(dx=dx))

    def stage(number, u):
        d, span = UNITS[u]
        block = (first, second, span[1])
        span = pl.ds(*span)
        if number == 0:
            core_half(u, (0, 2, 1, 3, 4)[u]).start()
        elif number == 1:
            core_half(u, u).wait_recv()
            for dx in range(RING):
                zs[d, dx, :, span] = acc[d, dx, 1, 0, :, span] + rb[d, (RING - dx) % RING, 1, :, span]
            for dx in range(RING):
                total = acc[d, dx, 0, 0, :, span] + rb[d, (RING - dx) % RING, 0, :, span]
                fin[d, dx, :, :, span] = total.reshape(block)
            z_half(u).start()
        else:
            z_half(u).wait_recv()
            for dx in (2, 1, 3, 0):
                total = fin[d, dx, :, :, span] + zr[d, dx, :, span].reshape(block)
                if dx == 0:
                    out_ref[:, :, home(u)] = total
                else:
                    fin[d, dx, :, :, span] = total
            for dx in (2, 1, 3):
                result(u, dx).start()

    def run(entry):
        op, m = entry
        if op == 2:
            stage(m[0], m[1])
        elif m[0] == XE:
            give(m[1], m[2]).start()
        elif op == 1:
            message(m).start()
        elif m[0] == LA:
            j = m[1] // 2
            if m[1] % 2:
                give(j, 0).wait_recv()
                give(j, 1).wait_recv()
            else:
                own(j).wait()
                give(j, 2).wait_recv()
        else:
            message(m).wait_recv()

    early = 0
    while STEPS[0][early][0] == 1:
        run(STEPS[0][early])
        early += 1
    for j in (0, 1, 3, 2):
        give(j, 2).start()
        own(j).start()
    for entry in STEPS[0][early:]:
        if entry[0] == 0 and entry[1][0] != LA:
            break
        run(entry)
        early += 1
    acc[...] = jnp.zeros_like(acc)
    for entry in STEPS[0][early:]:
        run(entry)

    @pl.loop(0, len(ORDER))
    def _(t):
        for number, group in enumerate(STEPS[:-1]):
            if group and number:

                @pl.when(t == number)
                def _():
                    for entry in group:
                        run(entry)

        dy, j = choose(t, [d for _, d, _ in ORDER]), choose(t, [b for _, _, b in ORDER])

        @pl.when(among(t, FRESH))
        def _():
            ah[j], al[j] = split(ag[j].reshape(ah.shape[1:]))

        for number, span in enumerate(SPANS):

            @pl.when(among(t, [n for n, (c, _, _) in enumerate(ORDER) if c == number]))
            def _():
                held = pl.ds(*span)
                high, low = split(vg[dy, j, :, held])
                product = jnp.dot(ah[j], high, preferred_element_type=jnp.float32)
                product += jnp.dot(ah[j], low, preferred_element_type=jnp.float32)
                product += jnp.dot(al[j], high, preferred_element_type=jnp.float32)
                acc[dy, :, :, :, :, held] += product.reshape(acc.shape[1:-1] + (span[1],))

    for entry in STEPS[-1]:
        run(entry)

    for u in range(len(UNITS)):
        core_half(u, u).wait_send()
        z_half(u).wait_send()
        for dx in (1, 2, 3):
            result(u, dx).wait()
    for j in range(RING):
        for way in (0, 1, 2):
            give(j, way).wait_send()
    for m in MESSAGES:
        message(m).wait_send()


def body(amplitudes, integrals, amp_pattern, int_pattern):
    first, second, depth = amplitudes.shape
    rows, width = integrals.shape
    pairs = first * second
    f32, bf16 = jnp.float32, jnp.bfloat16
    dma = pltpu.SemaphoreType.DMA
    units = len(UNITS)
    return pl.pallas_call(
        kernel,
        out_shape=jax.ShapeDtypeStruct((first, second, depth), f32),
        in_specs=[pl.BlockSpec(memory_space=pltpu.SMEM)] * 2 + [pl.BlockSpec(memory_space=pltpu.VMEM)] * 2,
        out_specs=pl.BlockSpec(memory_space=pltpu.VMEM),
        scratch_shapes=[
            pltpu.VMEM((first, second, depth), f32),
            pltpu.VMEM((RING, RING, rows, width), f32),
            pltpu.VMEM((RING, RING, 2, 2, first, second, width), f32),
            pltpu.VMEM((RING, RING * 4 * pairs, width), bf16),
            pltpu.VMEM((RING, RING * 4 * pairs, width), bf16),
            pltpu.VMEM((RING, RING, 2, 2, pairs, width), f32),
            pltpu.VMEM((RING, RING, 2, pairs, width), f32),
            pltpu.VMEM((RING, RING, pairs, width), f32),
            pltpu.VMEM((RING, RING, pairs, width), f32),
            pltpu.VMEM((RING, RING, first, second, width), f32),
            dma((len(MESSAGES),)),
            dma((len(MESSAGES),)),
            dma((RING,)),
            dma((RING, 3)),
            dma((RING, 3)),
            dma((units,)),
            dma((units,)),
            dma((units,)),
            dma((units,)),
            dma((units, RING)),
            dma((units, RING)),
        ],
        compiler_params=pltpu.CompilerParams(collective_id=0, has_side_effects=True, vmem_limit_bytes=60000 * 1024),
    )(amp_pattern, int_pattern, amplitudes, integrals)


def solution(mesh):
    placed = (P("col", "row", None), P("col", "row"), P("col", None), P(None, "row"))
    return jax.shard_map(
        body, mesh=mesh, in_specs=placed, out_specs=P("col", "row", None), check_vma=False
    )
```

```python
import jax
import jax.numpy as jnp
from jax import lax
from jax.experimental import pallas as pl
from jax.experimental.pallas import tpu as pltpu
from jax.sharding import PartitionSpec as P

TILE = 128
MESH = pl.DeviceIdType.MESH
RING, SZ = 4, 8
PARTS = 2
B1, B2, B3, XA, LA, XE, A1, A2 = range(8)
CUT = 32
FULL, WIDE, NARROW = (0, 384), (0, 256), (256, 128)
SPANS = (FULL, WIDE, NARROW)
UNITS = ((0, FULL), (1, FULL), (3, FULL), (2, WIDE), (2, NARROW))

PROGRAM = (
    (1153, 1793, 1157, 1797, 1664, 1668, 1029, 1037, 512, 1409, 1413, 528, 1425, 1429, 1025, 1672, 560, 1457, 1461,
     1161, 1165, 769, 1794, 520, 1417, 1421, 1925, 5, 1201, 1205, 385, 1410, 544, 1445, 129, 137, 1282, 1676, 1,
     1173, 1688, 401, 1426, 1169, 1692, 536, 1437, 1680, 393, 1418, 1933, 1684, 13, 1213, 773, 1949, 568, 1469,
     1033, 1209, 1433, 770, 1941, 1026, 552, 1453, 1465, 1290, 386, 389, 394, 397,),
    (),
    (433, 1458, 177, 185, 1330, 1921, 133, 141,),
    (409, 1434, 9, 1177, 1181, 258,),
    (266,),
    (441, 1466, 1441, 1034, 1338, 1929, 2, 1189, 1449, 897, 402, 405, 410, 413,),
    (901, 434, 437, 442, 445,),
    (417, 1442, 909,),
    (1185, 1922, 1945, 181, 189, 925,),
    (425, 1450, 10, 1193, 1197, 905, 1930, 145, 153,),
    (1937, 306, 917,),
    (921, 1946, 149, 157,),
    (913, 1938, 898, 418, 421, 426, 429,),
    (2048, 1298, 314,),
    (165, 173, 922,),
    (2064, 2176, 161, 169, 1314, 906,),
    (2056, 1306, 2184, 274,),
    (2192, 2304, 1322, 290, 914,),
    (2072, 2312, 282,),
    (2200, 298,),
    (2080, 2320, 2208, 2328, 2336,),
)
ORDER = ((0, 0, 0), (0, 1, 0), (0, 3, 0), (1, 2, 0), (2, 2, 0), (0, 0, 1), (0, 0, 3), (0, 1, 3), (0, 3, 3), (0, 1,
    1), (1, 2, 3), (0, 3, 1), (0, 0, 2), (2, 2, 3), (0, 3, 2), (0, 1, 2), (1, 2, 1), (1, 2, 2), (2, 2, 1), (2, 2,
    2))


def decode(code):
    code, hop = divmod(code, 4)
    code, direction = divmod(code, 2)
    code, index = divmod(code, 16)
    op, kind = divmod(code, 8)
    return op, (kind, index, direction, hop)


STEPS = tuple(tuple(decode(code) for code in group) for group in PROGRAM)
MESSAGES = tuple(sorted({m for group in STEPS for op, m in group if op == 1 and m[0] != XE}))
IDS = {m: n for n, m in enumerate(MESSAGES)}


def firsts(values):
    return tuple(min(n for n, v in enumerate(values) if v == value) for value in sorted(set(values)))


FRESH = firsts([b for _, _, b in ORDER])


def place(direction, hop):
    return hop if direction == 0 else (RING - hop) % RING


def split(value):
    high = value.astype(jnp.bfloat16)
    return high, (value - high.astype(jnp.float32)).astype(jnp.bfloat16)


def choose(t, values):
    chosen = jnp.int32(values[0])
    for number, value in enumerate(values[1:], 1):
        if value != values[number - 1]:
            chosen = jnp.where(t >= number, value, chosen)
    return chosen


def among(t, numbers):
    found = t == numbers[0]
    for number in numbers[1:]:
        found = jnp.logical_or(found, t == number)
    return found


def kernel(
    amp_hbm, int_hbm, a_hbm, v_hbm, out_ref, amp_ref, int_ref, am, vg, ag, ah, al, acc, rb, zs, zr, fin,
    isem, send, recv, lsem, xes, xer, r1s, r1r, r2s, r2r, r3s, r3r, ksem,
):
    row, col = lax.axis_index("row"), lax.axis_index("col")
    y, x = row // RING, row % RING
    z, k = col // 2, col % 2
    s = 1 - 2 * k
    first, second, depth = a_hbm.shape
    rows, width = v_hbm.shape
    pairs = first * second
    tiles = rows // TILE
    piece = (rows - CUT) // PARTS

    def device(dx=0, dy=0, dz=0, core=k):
        return (((y - s * dy + RING) % RING) * RING + (x - s * dx + RING) % RING, ((z - s * dz + SZ) % SZ) * 2 + core)

    sibling = device(core=1 - k)
    ahead, behind, across = device(dz=-1), device(dz=1), device(dz=-1, core=1 - k)

    loads = [
        pltpu.make_async_copy(source, target, isem.at[n])
        for n, (source, target) in enumerate(((int_hbm, int_ref), (v_hbm, vg.at[0, 0]), (amp_hbm, amp_ref), (a_hbm, am)))
    ]
    for load in loads:
        load.start()
    barrier = pltpu.get_barrier_semaphore()
    partners = [sibling, ahead, behind, across, device(dz=2), device(dz=-2)]
    partners += [device(dx=d) for d in (1, 2, 3)] + [device(dy=d) for d in (1, 3)]
    for partner in partners:
        pl.semaphore_signal(barrier, inc=1, device_id=partner, device_id_type=MESH)

    loads[0].wait()
    loads[1].wait()
    for r in range(tiles):
        for c in range(width // TILE):
            part = (0, 0, pl.ds(r * TILE, TILE), pl.ds(c * TILE, TILE))
            vg[part] = vg[part] * int_ref[c, col * tiles + r].astype(jnp.float32)

    loads[2].wait()
    loads[3].wait()

    @pl.loop(0, depth // TILE)
    def _(tile):
        part = pl.ds(pl.multiple_of(tile * TILE, TILE), TILE)
        for i in range(first):
            am[i, :, part] = am[i, :, part] * amp_ref[i, tile].astype(jnp.float32)

    pl.semaphore_wait(barrier, len(partners))

    def remote(source, target, send_sem, recv_sem, to):
        return pltpu.make_async_remote_copy(
            src_ref=source, dst_ref=target, send_sem=send_sem, recv_sem=recv_sem, device_id=to, device_id_type=MESH
        )

    def message(m):
        kind, index, direction, hop = m
        step = 1 if direction == 0 else -1
        here, there = place(direction, hop - 1), place(direction, hop)
        if kind == XA:
            block, foreign = index // 2, index % 2
            source, target, to = ag.at[block, here, foreign], ag.at[block, there, foreign], device(dx=-step)
        elif kind == B1:
            part = pl.ds(CUT + index * piece, piece)
            source, target, to = vg.at[0, here, part], vg.at[0, there, part], device(dz=-2 * step)
        elif kind == A1:
            part = pl.ds(0, CUT)
            source, target, to = vg.at[here, 0, part], vg.at[there, 0, part], device(dy=-step)
        elif kind == A2:
            part = pl.ds(0, CUT)
            source, target, to = vg.at[index, here, part], vg.at[index, there, part], device(dz=-2 * step)
        elif kind == B2:
            block, part = index // PARTS, pl.ds(CUT + index % PARTS * piece, piece)
            source, target, to = vg.at[here, block, part], vg.at[there, block, part], device(dy=-step)
        else:
            block, span = index // 2, pl.ds(*SPANS[1 + index % 2])
            rest = pl.ds(CUT, rows - CUT)
            source, target, to = vg.at[here, block, rest, span], vg.at[there, block, rest, span], device(dy=-step)
        return remote(source, target, send.at[IDS[m]], recv.at[IDS[m]], to)

    def columns(start, offset=0, size=None):
        return pl.ds(pl.multiple_of(start * width + offset, TILE), size or width)

    def block_of(owner, sense, core, j):
        return am.at[:, :, columns(2 * ((owner - sense * 2 * j + 2 * SZ) % SZ) + core)]

    def own(j):
        return pltpu.make_async_copy(block_of(z, s, k, j), ag.at[j, 0, 0, 0], lsem.at[j])

    def give(j, way):
        owner = z + s if way < 2 else z
        slot = ((1, 0), (1, 1), (0, 1))[way]
        sense, core = (s, k) if way == 0 else (-s, 1 - k)
        to = (ahead, across, sibling)[way]
        return remote(block_of(owner, sense, core, j), ag.at[(j, 0) + slot], xes.at[j, way], xer.at[j, way], to)

    def core_half(u, there):
        d, span = UNITS[u]
        span = pl.ds(*span)
        return remote(acc.at[d, :, :, 1, :, span], rb.at[UNITS[there][0], :, :, :, span], r1s.at[u], r1r.at[there], sibling)

    def z_half(u):
        d, span = UNITS[u]
        span = pl.ds(*span)
        return remote(zs.at[d, :, :, span], zr.at[d, :, :, span], r2s.at[u], r2r.at[u], behind)

    def home(u):
        d, span = UNITS[u]
        return columns((y - s * d + RING) % RING * RING + x, *span)

    def result(u, dx):
        d, span = UNITS[u]
        return remote(fin.at[d, dx, :, :, pl.ds(*span)], out_ref.at[:, :, home(u)], r3s.at[u, dx], r3r.at[u, dx], device(dx=dx))

    def kept(u):
        d, span = UNITS[u]
        return pltpu.make_async_copy(fin.at[d, 0, :, :, pl.ds(*span)], out_ref.at[:, :, home(u)], ksem.at[u])

    def stage(number, u):
        d, span = UNITS[u]
        block = (first, second, span[1])
        span = pl.ds(*span)
        if number == 0:
            core_half(u, (0, 2, 1, 3, 4)[u]).start()
        elif number == 1:
            core_half(u, u).wait_recv()
            for dx in range(RING):
                zs[d, dx, :, span] = acc[d, dx, 1, 0, :, span] + rb[d, (RING - dx) % RING, 1, :, span]
            for dx in range(RING):
                total = acc[d, dx, 0, 0, :, span] + rb[d, (RING - dx) % RING, 0, :, span]
                fin[d, dx, :, :, span] = total.reshape(block)
            z_half(u).start()
        else:
            z_half(u).wait_recv()
            for dx in (2, 1, 3, 0):
                total = fin[d, dx, :, :, span] + zr[d, dx, :, span].reshape(block)
                fin[d, dx, :, :, span] = total
            for dx in (2, 1, 3):
                result(u, dx).start()
            kept(u).start()

    def run(entry):
        op, m = entry
        if op == 2:
            stage(m[0], m[1])
        elif m[0] == XE:
            give(m[1], m[2]).start()
        elif op == 1:
            message(m).start()
        elif m[0] == LA:
            j = m[1] // 2
            if m[1] % 2:
                give(j, 0).wait_recv()
                give(j, 1).wait_recv()
            else:
                own(j).wait()
                give(j, 2).wait_recv()
        else:
            message(m).wait_recv()

    early = 0
    while STEPS[0][early][0] == 1:
        run(STEPS[0][early])
        early += 1
    for j in (0, 1, 3, 2):
        give(j, 2).start()
        own(j).start()
    for entry in STEPS[0][early:]:
        if entry[0] == 0 and entry[1][0] != LA:
            break
        run(entry)
        early += 1
    acc[...] = jnp.zeros_like(acc)
    for entry in STEPS[0][early:]:
        run(entry)

    @pl.loop(0, len(ORDER))
    def _(t):
        for number, group in enumerate(STEPS[:-1]):
            if group and number:

                @pl.when(t == number)
                def _():
                    for entry in group:
                        run(entry)

        dy, j = choose(t, [d for _, d, _ in ORDER]), choose(t, [b for _, _, b in ORDER])

        @pl.when(among(t, FRESH))
        def _():
            ah[j], al[j] = split(ag[j].reshape(ah.shape[1:]))

        for number, span in enumerate(SPANS):

            @pl.when(among(t, [n for n, (c, _, _) in enumerate(ORDER) if c == number]))
            def _():
                held = pl.ds(*span)
                high, low = split(vg[dy, j, :, held])
                product = jnp.dot(ah[j], high, preferred_element_type=jnp.float32)
                product += jnp.dot(ah[j], low, preferred_element_type=jnp.float32)
                product += jnp.dot(al[j], high, preferred_element_type=jnp.float32)
                acc[dy, :, :, :, :, held] += product.reshape(acc.shape[1:-1] + (span[1],))

    for entry in STEPS[-1]:
        run(entry)

    for u in range(len(UNITS)):
        core_half(u, u).wait_send()
        z_half(u).wait_send()
        for dx in (1, 2, 3):
            result(u, dx).wait()
        kept(u).wait()
    for j in range(RING):
        for way in (0, 1, 2):
            give(j, way).wait_send()
    for m in MESSAGES:
        message(m).wait_send()


def body(amplitudes, integrals, amp_pattern, int_pattern):
    first, second, depth = amplitudes.shape
    rows, width = integrals.shape
    pairs = first * second
    f32, bf16 = jnp.float32, jnp.bfloat16
    dma = pltpu.SemaphoreType.DMA
    units = len(UNITS)
    return pl.pallas_call(
        kernel,
        out_shape=pltpu.VMEM((first, second, depth), f32),
        in_specs=[pl.BlockSpec(memory_space=pl.ANY)] * 4,
        out_specs=pl.BlockSpec(memory_space=pl.ANY),
        scratch_shapes=[
            pltpu.SMEM(amp_pattern.shape, jnp.int32),
            pltpu.SMEM(int_pattern.shape[::-1], jnp.int32),
            pltpu.VMEM((first, second, depth), f32),
            pltpu.VMEM((RING, RING, rows, width), f32),
            pltpu.VMEM((RING, RING, 2, 2, first, second, width), f32),
            pltpu.VMEM((RING, RING * 4 * pairs, width), bf16),
            pltpu.VMEM((RING, RING * 4 * pairs, width), bf16),
            pltpu.VMEM((RING, RING, 2, 2, pairs, width), f32),
            pltpu.VMEM((RING, RING, 2, pairs, width), f32),
            pltpu.VMEM((RING, RING, pairs, width), f32),
            pltpu.VMEM((RING, RING, pairs, width), f32),
            pltpu.VMEM((RING, RING, first, second, width), f32),
            dma((4,)),
            dma((len(MESSAGES),)),
            dma((len(MESSAGES),)),
            dma((RING,)),
            dma((RING, 3)),
            dma((RING, 3)),
            dma((units,)),
            dma((units,)),
            dma((units,)),
            dma((units,)),
            dma((units, RING)),
            dma((units, RING)),
            dma((units,)),
        ],
        compiler_params=pltpu.CompilerParams(collective_id=0, has_side_effects=True, vmem_limit_bytes=46000 * 1024),
    )(*(pltpu.with_memory_space_constraint(o, pltpu.HBM) for o in (amp_pattern, int_pattern.T, amplitudes, integrals)))


def solution(mesh):
    placed = (P("col", "row", None), P("col", "row"), P("col", None), P(None, "row"))
    return jax.shard_map(
        body, mesh=mesh, in_specs=placed, out_specs=P("col", "row", None), check_vma=False
    )
```

```python
import jax
import jax.numpy as jnp
from jax import lax
from jax.experimental import pallas as pl
from jax.experimental.pallas import tpu as pltpu
from jax.sharding import PartitionSpec as P

TILE = 128
MESH = pl.DeviceIdType.MESH
RING, SZ = 4, 8
PARTS = 2
B1, B2, B3, XA, LA, XE, A1, A2 = range(8)
CUT = 32
FULL, WIDE, NARROW = (0, 384), (0, 256), (256, 128)
SPANS = (FULL, WIDE, NARROW)
UNITS = ((0, (0, 384)), (1, (0, 384)), (3, (0, 384)), (2, (0, 256)), (2, (256, 128)))
MIRROR = tuple(UNITS.index(((RING - d) % RING, span)) for d, span in UNITS)

PROGRAM = (
    (1153, 1161, 1157, 1165, 1664, 1668, 1029, 1037, 512, 1409, 1413, 528, 1425, 1429, 1025, 1672, 560, 1457, 1461,
     1793, 1797, 520, 1417, 1421, 1925, 5, 1201, 129, 137, 1282, 1205, 385, 1410, 544, 1445, 1676, 1, 1173, 1688,
     401, 1426, 1169, 1692, 536, 1437, 1033, 393, 1418, 769, 1933, 386, 389,),
    (13, 1213, 1026,),
    (568, 1469, 773, 1949, 133, 141,),
    (1433, 1794, 1465, 1209, 1290, 394, 397,),
    (433, 1458, 1680, 770, 1941,),
    (9, 1181,),
    (409, 1434, 1177, 258,),
    (),
    (441, 1466, 177, 185, 1330, 901, 434, 437,),
    (1441, 1684, 909,),
    (1034, 181, 189, 925,),
    (2, 1189, 1921, 266,),
    (),
    (1185, 552, 1449, 1453, 442, 445,),
    (),
    (),
    (417, 1442, 1929, 1945, 10, 1197, 1193, 1937, 425, 1450, 897, 410, 413,),
    (1922, 402, 405,),
    (905, 1930, 145, 153,),
    (921, 1946, 149, 157,),
    (913, 1938,),
    (898, 426, 429,),
    (2048, 1298, 418, 421,),
    (2304, 165, 173, 922,),
    (2064, 2176, 1306,),
    (),
    (2320, 161, 169, 906,),
    (2056, 2184,),
    (2312, 1314, 306, 917,),
    (2192, 274,),
    (2432, 1338,),
    (),
    (282,),
    (),
    (1322, 2440, 290, 914,),
    (2072,),
    (2328, 314,),
    (2200,),
    (2448, 298,),
    (2080,),
    (2336, 2208, 2456, 2464,),
)
ORDER = ((0, 0, 0, 0), (0, 1, 0, 0), (0, 3, 0, 0), (0, 0, 0, 1), (0, 1, 0, 1), (0, 3, 0, 1), (1, 2, 0, 1), (1, 2, 0,
    0), (0, 0, 3, 0), (0, 1, 3, 0), (0, 3, 3, 0), (2, 2, 0, 1), (2, 2, 0, 0), (0, 0, 3, 1), (0, 1, 3, 1), (0, 3, 3,
    1), (0, 0, 1, 1), (0, 0, 1, 0), (0, 1, 1, 1), (0, 3, 1, 1), (0, 1, 1, 0), (0, 0, 2, 1), (0, 0, 2, 0), (0, 3, 2,
    1), (0, 3, 1, 0), (0, 3, 2, 0), (0, 1, 2, 1), (0, 1, 2, 0), (1, 2, 3, 1), (1, 2, 1, 1), (1, 2, 1, 0), (1, 2, 3,
    0), (2, 2, 1, 1), (2, 2, 1, 0), (1, 2, 2, 1), (1, 2, 2, 0), (2, 2, 3, 1), (2, 2, 3, 0), (2, 2, 2, 1), (2, 2, 2,
    0))


def decode(code):
    code, hop = divmod(code, 4)
    code, direction = divmod(code, 2)
    code, index = divmod(code, 16)
    op, kind = divmod(code, 8)
    return op, (kind, index, direction, hop)


STEPS = tuple(tuple(decode(code) for code in group) for group in PROGRAM)
MESSAGES = tuple(sorted({m for group in STEPS for op, m in group if op == 1 and m[0] != XE}))
IDS = {m: n for n, m in enumerate(MESSAGES)}


def firsts(values):
    return tuple(min(n for n, v in enumerate(values) if v == value) for value in sorted(set(values)))


FRESH = firsts([b * 2 + a for _, _, b, a in ORDER])


def place(direction, hop):
    return hop if direction == 0 else (RING - hop) % RING


def split(value):
    high = value.astype(jnp.bfloat16)
    return high, (value - high.astype(jnp.float32)).astype(jnp.bfloat16)


def choose(t, values):
    words = [sum(v << (2 * n) for n, v in enumerate(values[w : w + 15])) for w in range(0, len(values), 15)]
    word = jnp.int32(words[0])
    for number, value in enumerate(words[1:], 1):
        word = jnp.where(t >= 15 * number, value, word)
    return lax.shift_right_logical(word, 2 * (t % 15)) & 3


def at_step(t, actions, width=7):
    for low in range(0, len(actions), width):
        group = [(n, act) for n, act in enumerate(actions[low : low + width], low) if act]
        if group:

            @pl.when(jnp.logical_and(t >= low, t < low + width))
            def _():
                for number, act in group:
                    pl.when(t == number)(act)


def kernel(
    amp_hbm, int_hbm, a_hbm, v_hbm, out_ref, amp_ref, int_ref, am, vg, ag, ah, al, acc, rb, zs, zr, fin,
    isem, send, recv, lsem, xes, xer, r1s, r1r, r2s, r2r, r3s, r3r, ksem,
):
    row, col = lax.axis_index("row"), lax.axis_index("col")
    y, x = row // RING, row % RING
    z, k = col // 2, col % 2
    s = 1 - 2 * k
    first, second, depth = a_hbm.shape
    rows, width = v_hbm.shape
    pairs = first * second
    tiles = rows // TILE
    piece = (rows - CUT) // PARTS

    def device(dx=0, dy=0, dz=0, core=k):
        return (((y - s * dy + RING) % RING) * RING + (x - s * dx + RING) % RING, ((z - s * dz + SZ) % SZ) * 2 + core)

    sibling = device(core=1 - k)
    ahead, behind, across = device(dz=-1), device(dz=1), device(dz=-1, core=1 - k)

    loads = [
        pltpu.make_async_copy(source, target, isem.at[n])
        for n, (source, target) in enumerate(((int_hbm, int_ref), (v_hbm, vg.at[0, 0]), (amp_hbm, amp_ref), (a_hbm, am)))
    ]
    for load in loads:
        load.start()
    barrier = pltpu.get_barrier_semaphore()
    partners = [sibling, ahead, behind, across, device(dz=2), device(dz=-2)]
    partners += [device(dx=d) for d in (1, 2, 3)] + [device(dy=d) for d in (1, 3)]
    for partner in partners:
        pl.semaphore_signal(barrier, inc=1, device_id=partner, device_id_type=MESH)

    loads[0].wait()
    loads[1].wait()
    for r in range(tiles):
        for c in range(width // TILE):
            part = (0, 0, pl.ds(r * TILE, TILE), pl.ds(c * TILE, TILE))
            vg[part] = vg[part] * int_ref[c, col * tiles + r].astype(jnp.float32)

    loads[2].wait()
    loads[3].wait()

    @pl.loop(0, depth // TILE)
    def _(tile):
        part = pl.ds(pl.multiple_of(tile * TILE, TILE), TILE)
        for i in range(first):
            am[i, :, part] = am[i, :, part] * amp_ref[i, tile].astype(jnp.float32)

    pl.semaphore_wait(barrier, len(partners))

    def remote(source, target, send_sem, recv_sem, to):
        return pltpu.make_async_remote_copy(
            src_ref=source, dst_ref=target, send_sem=send_sem, recv_sem=recv_sem, device_id=to, device_id_type=MESH
        )

    def message(m):
        kind, index, direction, hop = m
        step = 1 if direction == 0 else -1
        here, there = place(direction, hop - 1), place(direction, hop)
        if kind == XA:
            block, foreign = index // 2, index % 2
            source, target, to = ag.at[block, here, foreign], ag.at[block, there, foreign], device(dx=-step)
        elif kind == B1:
            part = pl.ds(CUT + index * piece, piece)
            source, target, to = vg.at[0, here, part], vg.at[0, there, part], device(dz=-2 * step)
        elif kind == A1:
            part = pl.ds(0, CUT)
            source, target, to = vg.at[here, 0, part], vg.at[there, 0, part], device(dy=-step)
        elif kind == A2:
            part = pl.ds(0, CUT)
            source, target, to = vg.at[index, here, part], vg.at[index, there, part], device(dz=-2 * step)
        elif kind == B2:
            block, part = index // PARTS, pl.ds(CUT + index % PARTS * piece, piece)
            source, target, to = vg.at[here, block, part], vg.at[there, block, part], device(dy=-step)
        else:
            block, span = index // 2, pl.ds(*SPANS[1 + index % 2])
            rest = pl.ds(CUT, rows - CUT)
            source, target, to = vg.at[here, block, rest, span], vg.at[there, block, rest, span], device(dy=-step)
        return remote(source, target, send.at[IDS[m]], recv.at[IDS[m]], to)

    def columns(start, offset=0, size=None):
        return pl.ds(pl.multiple_of(start * width + offset, TILE), size or width)

    def block_of(owner, sense, core, j):
        return am.at[:, :, columns(2 * ((owner - sense * 2 * j + 2 * SZ) % SZ) + core)]

    def own(j):
        return pltpu.make_async_copy(block_of(z, s, k, j), ag.at[j, 0, 0, 0], lsem.at[j])

    def give(j, way):
        owner = z + s if way < 2 else z
        slot = ((1, 0), (1, 1), (0, 1))[way]
        sense, core = (s, k) if way == 0 else (-s, 1 - k)
        to = (ahead, across, sibling)[way]
        return remote(block_of(owner, sense, core, j), ag.at[(j, 0) + slot], xes.at[j, way], xer.at[j, way], to)

    def core_half(u, foreign, there):
        d, span = UNITS[u]
        span = pl.ds(*span)
        return remote(
            acc.at[d, foreign, :, 1, :, span],
            rb.at[UNITS[there][0], foreign, :, :, span],
            r1s.at[u, foreign],
            r1r.at[there, foreign],
            sibling,
        )

    def z_half(u):
        d, span = UNITS[u]
        span = pl.ds(*span)
        return remote(zs.at[d, :, :, span], zr.at[d, :, :, span], r2s.at[u], r2r.at[u], behind)

    def home(u):
        d, span = UNITS[u]
        return columns((y - s * d + RING) % RING * RING + x, *span)

    def result(u, dx):
        d, span = UNITS[u]
        return remote(fin.at[d, dx, :, :, pl.ds(*span)], out_ref.at[:, :, home(u)], r3s.at[u, dx], r3r.at[u, dx], device(dx=dx))

    def kept(u):
        d, span = UNITS[u]
        return pltpu.make_async_copy(fin.at[d, 0, :, :, pl.ds(*span)], out_ref.at[:, :, home(u)], ksem.at[u])

    def stage(number, u):
        d, span = UNITS[u]
        block = (first, second, span[1])
        span = pl.ds(*span)
        if number % 2 == 0:
            core_half(u, 1 - number // 2, MIRROR[u]).start()
        elif number == 1:
            core_half(u, 1, u).wait_recv()
            for dx in range(RING):
                zs[d, dx, :, span] = acc[d, 1, dx, 0, :, span] + rb[d, 1, (RING - dx) % RING, :, span]
            z_half(u).start()
        else:
            core_half(u, 0, u).wait_recv()
            z_half(u).wait_recv()
            for dx in (2, 1, 3, 0):
                total = acc[d, 0, dx, 0, :, span] + rb[d, 0, (RING - dx) % RING, :, span] + zr[d, dx, :, span]
                fin[d, dx, :, :, span] = total.reshape(block)
            for dx in (2, 1, 3):
                result(u, dx).start()
            kept(u).start()

    def run(entry):
        op, m = entry
        if op == 2:
            stage(m[0], m[1])
        elif m[0] == XE:
            give(m[1], m[2]).start()
        elif op == 1:
            message(m).start()
        elif m[0] == LA:
            j = m[1] // 2
            if m[1] % 2:
                give(j, 0).wait_recv()
                give(j, 1).wait_recv()
            else:
                own(j).wait()
                give(j, 2).wait_recv()
        else:
            message(m).wait_recv()

    early = 0
    while STEPS[0][early][0] == 1:
        run(STEPS[0][early])
        early += 1
    for j in (0, 1, 3, 2):
        give(j, 2).start()
        own(j).start()
    for entry in STEPS[0][early:]:
        if entry[0] == 0 and entry[1][0] != LA:
            break
        run(entry)
        early += 1
    acc[...] = jnp.zeros_like(acc)
    for entry in STEPS[0][early:]:
        run(entry)

    @pl.loop(0, len(ORDER))
    def _(t):
        def events(group):
            def act():
                for entry in group:
                    run(entry)

            return act

        at_step(t, [events(group) if group and number else None for number, group in enumerate(STEPS[:-1])])
        dy, j, foreign = (choose(t, [entry[n] for entry in ORDER]) for n in (1, 2, 3))

        @pl.when(choose(t, [int(n in FRESH) for n in range(len(ORDER))]) == 1)
        def _():
            value = ag[j, :, foreign]
            ah[j, foreign], al[j, foreign] = split(value.reshape(ah.shape[2:]))

        columns_of = choose(t, [entry[0] for entry in ORDER])
        for number, span in enumerate(SPANS):

            @pl.when(columns_of == number)
            def _():
                held = pl.ds(*span)
                high, low = split(vg[dy, j, :, held])
                product = jnp.dot(ah[j, foreign], high, preferred_element_type=jnp.float32)
                product += jnp.dot(ah[j, foreign], low, preferred_element_type=jnp.float32)
                product += jnp.dot(al[j, foreign], high, preferred_element_type=jnp.float32)
                acc[dy, foreign, :, :, :, held] += product.reshape(acc.shape[2:-1] + (span[1],))

    for entry in STEPS[-1]:
        run(entry)

    for u in range(len(UNITS)):
        core_half(u, 0, u).wait_send()
        core_half(u, 1, u).wait_send()
        z_half(u).wait_send()
        for dx in (1, 2, 3):
            result(u, dx).wait()
        kept(u).wait()
    for j in range(RING):
        for way in (0, 1, 2):
            give(j, way).wait_send()
    for m in MESSAGES:
        message(m).wait_send()


def body(amplitudes, integrals, amp_pattern, int_pattern):
    first, second, depth = amplitudes.shape
    rows, width = integrals.shape
    pairs = first * second
    f32, bf16 = jnp.float32, jnp.bfloat16
    dma = pltpu.SemaphoreType.DMA
    units = len(UNITS)
    return pl.pallas_call(
        kernel,
        out_shape=pltpu.VMEM((first, second, depth), f32),
        in_specs=[pl.BlockSpec(memory_space=pl.ANY)] * 4,
        out_specs=pl.BlockSpec(memory_space=pl.ANY),
        scratch_shapes=[
            pltpu.SMEM(amp_pattern.shape, jnp.int32),
            pltpu.SMEM(int_pattern.shape[::-1], jnp.int32),
            pltpu.VMEM((first, second, depth), f32),
            pltpu.VMEM((RING, RING, rows, width), f32),
            pltpu.VMEM((RING, RING, 2, 2, first, second, width), f32),
            pltpu.VMEM((RING, 2, RING * 2 * pairs, width), bf16),
            pltpu.VMEM((RING, 2, RING * 2 * pairs, width), bf16),
            pltpu.VMEM((RING, 2, RING, 2, pairs, width), f32),
            pltpu.VMEM((RING, 2, RING, pairs, width), f32),
            pltpu.VMEM((RING, RING, pairs, width), f32),
            pltpu.VMEM((RING, RING, pairs, width), f32),
            pltpu.VMEM((RING, RING, first, second, width), f32),
            dma((4,)),
            dma((len(MESSAGES),)),
            dma((len(MESSAGES),)),
            dma((RING,)),
            dma((RING, 3)),
            dma((RING, 3)),
            dma((units, 2)),
            dma((units, 2)),
            dma((units,)),
            dma((units,)),
            dma((units, RING)),
            dma((units, RING)),
            dma((units,)),
        ],
        compiler_params=pltpu.CompilerParams(collective_id=0, has_side_effects=True, vmem_limit_bytes=46000 * 1024),
    )(*(pltpu.with_memory_space_constraint(o, pltpu.HBM) for o in (amp_pattern, int_pattern.T, amplitudes, integrals)))


def solution(mesh):
    placed = (P("col", "row", None), P("col", "row"), P("col", None), P(None, "row"))
    return jax.shard_map(
        body, mesh=mesh, in_specs=placed, out_specs=P("col", "row", None), check_vma=False
    )
```

```python
import jax
import jax.numpy as jnp
from jax import lax
from jax.experimental import pallas as pl
from jax.experimental.pallas import tpu as pltpu
from jax.sharding import PartitionSpec as P

TILE = 128
MESH = pl.DeviceIdType.MESH
RING, SZ = 4, 8
PARTS = 2
B1, B2, B3, XA, LA, XE, A1, A2 = range(8)
CUT = 32
FULL, WIDE, NARROW = (0, 384), (0, 256), (256, 128)
SPANS = (FULL, WIDE, NARROW)
UNITS = ((0, (0, 384)), (1, (0, 384)), (3, (0, 384)), (2, (0, 256)), (2, (256, 128)))
MIRROR = tuple(UNITS.index(((RING - d) % RING, span)) for d, span in UNITS)

PROGRAM = (
    (1153, 1161, 1157, 1165, 1664, 1668, 1029, 1037, 512, 1409, 1413, 528, 1425, 1429, 1025, 1672, 560, 1457, 1461,
     1793, 1797, 520, 1417, 1421, 1925, 5, 1201, 129, 137, 1282, 1205, 385, 1410, 544, 1445, 1676, 1, 1173, 1688,
     401, 1426, 1169, 1692, 536, 1437, 1033, 393, 1418, 769, 1933, 386, 389,),
    (13, 1213, 1026,),
    (568, 1469, 773, 1949, 133, 141,),
    (1433, 1794, 1465, 1209, 1290, 394, 397,),
    (433, 1458, 1680, 770, 1941,),
    (9, 1181,),
    (409, 1434, 1177, 258,),
    (),
    (441, 1466, 177, 185, 1330, 901, 434, 437,),
    (1441, 1684, 909,),
    (1034, 181, 189, 925,),
    (2, 1189, 1921, 266,),
    (),
    (1185, 552, 1449, 1453, 442, 445,),
    (),
    (),
    (417, 1442, 1929, 1945, 10, 1197, 1193, 1937, 425, 1450, 897, 410, 413,),
    (1922, 402, 405,),
    (905, 1930, 145, 153,),
    (921, 1946, 149, 157,),
    (913, 1938,),
    (898, 426, 429,),
    (2048, 1298, 418, 421,),
    (2304, 165, 173, 922,),
    (2064, 2176, 1306,),
    (),
    (2320, 161, 169, 906,),
    (2056, 2184,),
    (2312, 1314, 306, 917,),
    (2192, 274,),
    (2432, 1338,),
    (),
    (282,),
    (),
    (1322, 2440, 290, 914,),
    (2072,),
    (2328, 314,),
    (2200,),
    (2448, 298,),
    (2080,),
    (2336, 2208, 2456, 2464,),
)
ORDER = ((0, 0, 0, 0), (0, 1, 0, 0), (0, 3, 0, 0), (0, 0, 0, 1), (0, 1, 0, 1), (0, 3, 0, 1), (1, 2, 0, 1), (1, 2, 0,
    0), (0, 0, 3, 0), (0, 1, 3, 0), (0, 3, 3, 0), (2, 2, 0, 1), (2, 2, 0, 0), (0, 0, 3, 1), (0, 1, 3, 1), (0, 3, 3,
    1), (0, 0, 1, 1), (0, 0, 1, 0), (0, 1, 1, 1), (0, 3, 1, 1), (0, 1, 1, 0), (0, 0, 2, 1), (0, 0, 2, 0), (0, 3, 2,
    1), (0, 3, 1, 0), (0, 3, 2, 0), (0, 1, 2, 1), (0, 1, 2, 0), (1, 2, 3, 1), (1, 2, 1, 1), (1, 2, 1, 0), (1, 2, 3,
    0), (2, 2, 1, 1), (2, 2, 1, 0), (1, 2, 2, 1), (1, 2, 2, 0), (2, 2, 3, 1), (2, 2, 3, 0), (2, 2, 2, 1), (2, 2, 2,
    0))


def decode(code):
    code, hop = divmod(code, 4)
    code, direction = divmod(code, 2)
    code, index = divmod(code, 16)
    op, kind = divmod(code, 8)
    return op, (kind, index, direction, hop)


STEPS = tuple(tuple(decode(code) for code in group) for group in PROGRAM)
MESSAGES = tuple(sorted({m for group in STEPS for op, m in group if op == 1 and m[0] != XE}))
IDS = {m: n for n, m in enumerate(MESSAGES)}


def firsts(values):
    return tuple(min(n for n, v in enumerate(values) if v == value) for value in sorted(set(values)))


FRESH = firsts([b * 2 + a for _, _, b, a in ORDER])


def place(direction, hop):
    return hop if direction == 0 else (RING - hop) % RING


def split(value):
    high = value.astype(jnp.bfloat16)
    return high, (value - high.astype(jnp.float32)).astype(jnp.bfloat16)


def choose(t, values):
    words = [sum(v << (2 * n) for n, v in enumerate(values[w : w + 15])) for w in range(0, len(values), 15)]
    word = jnp.int32(words[0])
    for number, value in enumerate(words[1:], 1):
        word = jnp.where(t >= 15 * number, value, word)
    return lax.shift_right_logical(word, 2 * (t % 15)) & 3


def at_step(t, actions, width=7):
    for low in range(0, len(actions), width):
        group = [(n, act) for n, act in enumerate(actions[low : low + width], low) if act]
        if group:

            @pl.when(jnp.logical_and(t >= low, t < low + width))
            def _():
                for number, act in group:
                    pl.when(t == number)(act)


def kernel(
    amp_hbm, int_hbm, a_hbm, v_hbm, out_ref, amp_ref, int_ref, am, vg, ag, ah, al, acc, rb, zs, zr, fin,
    isem, send, recv, lsem, xes, xer, r1s, r1r, r2s, r2r, r3s, r3r, ksem,
):
    row, col = lax.axis_index("row"), lax.axis_index("col")
    y, x = row // RING, row % RING
    z, k = col // 2, col % 2
    s = 1 - 2 * k
    first, second, depth = a_hbm.shape
    rows, width = v_hbm.shape
    pairs = first * second
    tiles = rows // TILE
    piece = (rows - CUT) // PARTS

    def device(dx=0, dy=0, dz=0, core=k):
        return (((y - s * dy + RING) % RING) * RING + (x - s * dx + RING) % RING, ((z - s * dz + SZ) % SZ) * 2 + core)

    sibling = device(core=1 - k)
    ahead, behind, across = device(dz=-1), device(dz=1), device(dz=-1, core=1 - k)

    loads = [
        pltpu.make_async_copy(source, target, isem.at[n])
        for n, (source, target) in enumerate(((int_hbm, int_ref), (v_hbm, vg.at[0, 0]), (amp_hbm, amp_ref), (a_hbm, am)))
    ]
    for load in loads:
        load.start()
    barrier = pltpu.get_barrier_semaphore()
    partners = [sibling, ahead, behind, across, device(dz=2), device(dz=-2)]
    partners += [device(dx=d) for d in (1, 2, 3)] + [device(dy=d) for d in (1, 3)]
    for partner in partners:
        pl.semaphore_signal(barrier, inc=1, device_id=partner, device_id_type=MESH)

    loads[0].wait()
    loads[1].wait()
    for r in range(tiles):
        for c in range(width // TILE):
            part = (0, 0, pl.ds(r * TILE, TILE), pl.ds(c * TILE, TILE))
            vg[part] = vg[part] * int_ref[c, col * tiles + r].astype(jnp.float32)

    loads[2].wait()
    loads[3].wait()

    @pl.loop(0, depth // TILE)
    def _(tile):
        part = pl.ds(pl.multiple_of(tile * TILE, TILE), TILE)
        for i in range(first):
            am[i, :, part] = am[i, :, part] * amp_ref[i, tile].astype(jnp.float32)

    pl.semaphore_wait(barrier, len(partners))

    def remote(source, target, send_sem, recv_sem, to):
        return pltpu.make_async_remote_copy(
            src_ref=source, dst_ref=target, send_sem=send_sem, recv_sem=recv_sem, device_id=to, device_id_type=MESH
        )

    def message(m):
        kind, index, direction, hop = m
        step = 1 if direction == 0 else -1
        here, there = place(direction, hop - 1), place(direction, hop)
        if kind == XA:
            block, foreign = index // 2, index % 2
            source, target, to = ag.at[block, here, foreign], ag.at[block, there, foreign], device(dx=-step)
        elif kind == B1:
            part = pl.ds(CUT + index * piece, piece)
            source, target, to = vg.at[0, here, part], vg.at[0, there, part], device(dz=-2 * step)
        elif kind == A1:
            part = pl.ds(0, CUT)
            source, target, to = vg.at[here, 0, part], vg.at[there, 0, part], device(dy=-step)
        elif kind == A2:
            part = pl.ds(0, CUT)
            source, target, to = vg.at[index, here, part], vg.at[index, there, part], device(dz=-2 * step)
        elif kind == B2:
            block, part = index // PARTS, pl.ds(CUT + index % PARTS * piece, piece)
            source, target, to = vg.at[here, block, part], vg.at[there, block, part], device(dy=-step)
        else:
            block, span = index // 2, pl.ds(*SPANS[1 + index % 2])
            rest = pl.ds(CUT, rows - CUT)
            source, target, to = vg.at[here, block, rest, span], vg.at[there, block, rest, span], device(dy=-step)
        return remote(source, target, send.at[IDS[m]], recv.at[IDS[m]], to)

    def columns(start, offset=0, size=None):
        return pl.ds(pl.multiple_of(start * width + offset, TILE), size or width)

    def block_of(owner, sense, core, j):
        return am.at[:, :, columns(2 * ((owner - sense * 2 * j + 2 * SZ) % SZ) + core)]

    def own(j):
        return pltpu.make_async_copy(block_of(z, s, k, j), ag.at[j, 0, 0, 0], lsem.at[j])

    def give(j, way):
        owner = z + s if way < 2 else z
        slot = ((1, 0), (1, 1), (0, 1))[way]
        sense, core = (s, k) if way == 0 else (-s, 1 - k)
        to = (ahead, across, sibling)[way]
        return remote(block_of(owner, sense, core, j), ag.at[(j, 0) + slot], xes.at[j, way], xer.at[j, way], to)

    def core_half(u, foreign, there):
        d, span = UNITS[u]
        span = pl.ds(*span)
        return remote(
            acc.at[d, foreign, :, 1, :, span],
            rb.at[UNITS[there][0], foreign, :, :, span],
            r1s.at[u, foreign],
            r1r.at[there, foreign],
            sibling,
        )

    def z_half(u):
        d, span = UNITS[u]
        span = pl.ds(*span)
        return remote(zs.at[d, :, :, span], zr.at[d, :, :, span], r2s.at[u], r2r.at[u], behind)

    def home(u):
        d, span = UNITS[u]
        return columns((y - s * d + RING) % RING * RING + x, *span)

    def result(u, dx):
        d, span = UNITS[u]
        return remote(fin.at[d, dx, :, :, pl.ds(*span)], out_ref.at[:, :, home(u)], r3s.at[u, dx], r3r.at[u, dx], device(dx=dx))

    def kept(u):
        d, span = UNITS[u]
        return pltpu.make_async_copy(fin.at[d, 0, :, :, pl.ds(*span)], out_ref.at[:, :, home(u)], ksem.at[u])

    def stage(number, u):
        d, span = UNITS[u]
        block = (first, second, span[1])
        span = pl.ds(*span)
        if number % 2 == 0:
            core_half(u, 1 - number // 2, MIRROR[u]).start()
        elif number == 1:
            core_half(u, 1, u).wait_recv()
            for dx in range(RING):
                zs[d, dx, :, span] = acc[d, 1, dx, 0, :, span] + rb[d, 1, (RING - dx) % RING, :, span]
            z_half(u).start()
        else:
            core_half(u, 0, u).wait_recv()
            z_half(u).wait_recv()
            for dx in (2, 1, 3, 0):
                total = acc[d, 0, dx, 0, :, span] + rb[d, 0, (RING - dx) % RING, :, span] + zr[d, dx, :, span]
                fin[d, dx, :, :, span] = total.reshape(block)
            for dx in (2, 1, 3):
                result(u, dx).start()
            kept(u).start()

    def run(entry):
        op, m = entry
        if op == 2:
            stage(m[0], m[1])
        elif m[0] == XE:
            give(m[1], m[2]).start()
        elif op == 1:
            message(m).start()
        elif m[0] == LA:
            j = m[1] // 2
            if m[1] % 2:
                give(j, 0).wait_recv()
                give(j, 1).wait_recv()
            else:
                own(j).wait()
                give(j, 2).wait_recv()
        else:
            message(m).wait_recv()

    early = 0
    while STEPS[0][early][0] == 1:
        run(STEPS[0][early])
        early += 1
    for j in (0, 1, 3, 2):
        give(j, 2).start()
        own(j).start()
    for entry in STEPS[0][early:]:
        if entry[0] == 0 and entry[1][0] != LA:
            break
        run(entry)
        early += 1
    acc[...] = jnp.zeros_like(acc)
    for entry in STEPS[0][early:]:
        run(entry)

    @pl.loop(0, len(ORDER))
    def _(t):
        def events(group):
            def act():
                for entry in group:
                    run(entry)

            return act

        at_step(t, [events(group) if group and number else None for number, group in enumerate(STEPS[:-1])])
        dy, j, foreign = (choose(t, [entry[n] for entry in ORDER]) for n in (1, 2, 3))

        @pl.when(choose(t, [int(n in FRESH) for n in range(len(ORDER))]) == 1)
        def _():
            value = ag[j, :, foreign]
            ah[j, foreign], al[j, foreign] = split(value.reshape(ah.shape[2:]))

        columns_of = choose(t, [entry[0] for entry in ORDER])
        for number, span in enumerate(SPANS):

            @pl.when(columns_of == number)
            def _():
                held = pl.ds(*span)
                high, low = split(vg[dy, j, :, held])
                left = jnp.concatenate([ah[j, foreign], al[j, foreign], ah[j, foreign]], axis=1)
                product = jnp.dot(left, jnp.concatenate([high, high, low], axis=0), preferred_element_type=jnp.float32)
                acc[dy, foreign, :, :, :, held] += product.reshape(acc.shape[2:-1] + (span[1],))

    for entry in STEPS[-1]:
        run(entry)

    for u in range(len(UNITS)):
        core_half(u, 0, u).wait_send()
        core_half(u, 1, u).wait_send()
        z_half(u).wait_send()
        for dx in (1, 2, 3):
            result(u, dx).wait()
        kept(u).wait()
    for j in range(RING):
        for way in (0, 1, 2):
            give(j, way).wait_send()
    for m in MESSAGES:
        message(m).wait_send()


def body(amplitudes, integrals, amp_pattern, int_pattern):
    first, second, depth = amplitudes.shape
    rows, width = integrals.shape
    pairs = first * second
    f32, bf16 = jnp.float32, jnp.bfloat16
    dma = pltpu.SemaphoreType.DMA
    units = len(UNITS)
    return pl.pallas_call(
        kernel,
        out_shape=pltpu.VMEM((first, second, depth), f32),
        in_specs=[pl.BlockSpec(memory_space=pl.ANY)] * 4,
        out_specs=pl.BlockSpec(memory_space=pl.ANY),
        scratch_shapes=[
            pltpu.SMEM(amp_pattern.shape, jnp.int32),
            pltpu.SMEM(int_pattern.shape[::-1], jnp.int32),
            pltpu.VMEM((first, second, depth), f32),
            pltpu.VMEM((RING, RING, rows, width), f32),
            pltpu.VMEM((RING, RING, 2, 2, first, second, width), f32),
            pltpu.VMEM((RING, 2, RING * 2 * pairs, width), bf16),
            pltpu.VMEM((RING, 2, RING * 2 * pairs, width), bf16),
            pltpu.VMEM((RING, 2, RING, 2, pairs, width), f32),
            pltpu.VMEM((RING, 2, RING, pairs, width), f32),
            pltpu.VMEM((RING, RING, pairs, width), f32),
            pltpu.VMEM((RING, RING, pairs, width), f32),
            pltpu.VMEM((RING, RING, first, second, width), f32),
            dma((4,)),
            dma((len(MESSAGES),)),
            dma((len(MESSAGES),)),
            dma((RING,)),
            dma((RING, 3)),
            dma((RING, 3)),
            dma((units, 2)),
            dma((units, 2)),
            dma((units,)),
            dma((units,)),
            dma((units, RING)),
            dma((units, RING)),
            dma((units,)),
        ],
        compiler_params=pltpu.CompilerParams(collective_id=0, has_side_effects=True, vmem_limit_bytes=46000 * 1024),
    )(*(pltpu.with_memory_space_constraint(o, pltpu.HBM) for o in (amp_pattern, int_pattern.T, amplitudes, integrals)))


def solution(mesh):
    placed = (P("col", "row", None), P("col", "row"), P("col", None), P(None, "row"))
    return jax.shard_map(
        body, mesh=mesh, in_specs=placed, out_specs=P("col", "row", None), check_vma=False
    )
```
